32 devices in a mesh: scene: 4 (over y, core), seq: 8 (over z, x).
Axes of the slice: x: 2, y: 2, z: 4, core: 2. Of those that a mesh axis runs over, the one named last changes fastest.
Arguments:
- points: bfloat16 [32768, 256], P(('scene', 'seq')), may hold values from -100 to 100
- serial_rank: int32 [32768], P(('scene', 'seq')), may hold values from 0 to 8191, as said below
- mask_bits: int32 [12, 32768], P(None, ('scene', 'seq')), may hold values from 0 to 262143, as said below
- qkv_weight: bfloat16 [256, 768], replicated, may hold values from -2 to 2
- proj_weight: bfloat16 [256, 256], replicated, may hold values from -0.375 to 0.375
- up_weight: bfloat16 [256, 1024], replicated, may hold values from -0.375 to 0.375
- down_weight: bfloat16 [1024, 256], replicated, may hold values from -0.1875 to 0.1875
- queries: bfloat16 [200, 256], replicated, may hold values from -5 to 5
- dec_q_weight: bfloat16 [256, 256], replicated, may hold values from -3 to 3
- dec_kv_weight: bfloat16 [256, 512], replicated, may hold values from -2 to 2
- dec_out_weight: bfloat16 [256, 256], replicated, may hold values from -0.375 to 0.375
- mask_weight: bfloat16 [256, 256], replicated, may hold values from -0.375 to 0.375
Outputs:
- reserialized: bfloat16 [32768, 256], P(('scene', 'seq'))
- updated_queries: float32 [200, 256], replicated
- mask_logits: bfloat16 [200, 32768], P(None, ('scene', 'seq'))
The draws below stay inside these ranges and needn't reach their ends.
Inputs may be any that keep to these rules, and one draw needn't show every extreme that they name: Within each scene group of 8192 points, serial_rank is a permutation of 0 to 8191. The points of one device have at most 256 ranks in any one range k * 1024 to (k + 1) * 1024 - 1, and in every draw that most is reached. `mask_bits`: word w holds the bits of queries 18 * w to 18 * w + 17 (the last word those that remain). In every block of 1024 points each query may attend to at least one point.
All inputs are finite; a program needn't handle non-finite values.
Results may differ from the reference program's by a relative error of at most 0.015.
Values may be sent and summed in bfloat16 or wider, within the bound.
A program may use at most 192 MiB of HBM per device.

```python
import math
import jax
import jax.numpy as jnp
from jax import lax

C = 256
HEADS = 16
HDIM = 16
FF = 1024
PATCH = 1024
QUERIES = 200
DHEADS = 8
DHDIM = 32
WORDS = 12
P_DEV = 1024
GP = 8192
NPTS = 32768
N_SCENE = 4
N_SEQ = 8


def spread(key, shape, lower, upper):
    return jnp.exp(jax.random.uniform(key, shape, jnp.float32, math.log(lower), math.log(upper)))


def draw_points(key, part):
    noise_key, row_key, column_key = jax.random.split(jax.random.fold_in(key, 101), 3)
    noise = jnp.clip(jax.random.normal(noise_key, (NPTS, C), jnp.float32), -5.0, 5.0)
    row_scale = spread(row_key, (NPTS,), 0.3, 3.0)
    column_scale = spread(column_key, (C,), 0.3, 3.0)
    field = noise * row_scale[:, None] * column_scale[None, :]
    return field.astype(jnp.bfloat16)


def draw_queries(key, part):
    noise_key = jax.random.fold_in(jax.random.fold_in(key, 202), 0)
    field = jnp.clip(jax.random.normal(noise_key, (QUERIES, C), jnp.float32), -4.0, 4.0)
    return field.astype(jnp.bfloat16)


def random_matrix(key, shape):
    return jnp.clip(jax.random.normal(key, shape, jnp.float32), -4.0, 4.0)


def draw_qkv_weight(key, part):
    noise = random_matrix(jax.random.fold_in(key, 303), (C, 3 * C))
    columns = jnp.arange(3 * C)
    scales = jnp.where(columns < 2 * C, math.sqrt(3.0), 1.0) / math.sqrt(C)
    matrix = noise * scales[None, :]
    return matrix.astype(jnp.bfloat16)


def draw_dec_q_weight(key, part):
    matrix = random_matrix(jax.random.fold_in(key, 404), (C, C)) * (math.sqrt(12.0) / math.sqrt(C))
    return matrix.astype(jnp.bfloat16)


def draw_dec_kv_weight(key, part):
    matrix = random_matrix(jax.random.fold_in(key, 505), (C, 2 * C)) * (1.0 / math.sqrt(C))
    return matrix.astype(jnp.bfloat16)


def draw_serial_rank(key, part):
    share = P_DEV // N_SEQ

    def one_group(group_key):
        size_key, offset_key, source_key, target_key = jax.random.split(group_key, 4)
        amounts = jax.random.randint(size_key, (N_SEQ // 2 - 1,), 0, share).astype(jnp.int32)
        paired = jnp.stack([share + amounts, share - amounts], axis=1).reshape(-1)
        sizes = jnp.concatenate([jnp.array([2 * share, 0], jnp.int32), paired.astype(jnp.int32)])
        sizes = sizes[jax.random.permutation(offset_key, N_SEQ)]
        sources = jnp.arange(N_SEQ, dtype=jnp.int32)[:, None]
        targets = jnp.arange(N_SEQ, dtype=jnp.int32)[None, :]
        counts = sizes[(targets - sources) % N_SEQ]
        send_start = jnp.cumsum(counts, axis=1) - counts
        recv_start = jnp.cumsum(counts, axis=0) - counts
        ends = send_start + counts
        positions = jnp.arange(P_DEV, dtype=jnp.int32)
        label = jnp.sum((positions[None, :, None] >= ends[:, None, :]).astype(jnp.int32), axis=2)
        within = positions[None, :] - jnp.take_along_axis(send_start, label, axis=1)
        slot_index = jnp.take_along_axis(recv_start, label, axis=1) + within
        source_perms = jax.vmap(lambda inner: jax.random.permutation(inner, P_DEV))(jax.random.split(source_key, N_SEQ)).astype(jnp.int32)
        target_perms = jax.vmap(lambda inner: jax.random.permutation(inner, P_DEV))(jax.random.split(target_key, N_SEQ)).astype(jnp.int32)
        ranks = label * P_DEV + target_perms[label, slot_index]
        placed = jnp.zeros((N_SEQ, P_DEV), jnp.int32).at[jnp.arange(N_SEQ, dtype=jnp.int32)[:, None], source_perms].set(ranks)
        return placed.reshape(-1)
    group_keys = jax.random.split(jax.random.fold_in(key, 606), N_SCENE)
    return jax.vmap(one_group)(group_keys).reshape(-1).astype(jnp.int32)


def draw_mask_bits(key, part):
    rows_list = []
    for word_index in range(WORDS):
        used = min(18, QUERIES - 18 * word_index)
        rows_list.append(jax.random.randint(jax.random.fold_in(key, 710 + word_index), (NPTS,), 0, 2 ** used).astype(jnp.int32))
    packed = jnp.stack(rows_list, axis=0)
    first_used = min(18, QUERIES)
    packed = packed.at[0, 0].set(jnp.int32(2 ** first_used - 1))
    block_count = NPTS // P_DEV
    chosen = jax.random.randint(jax.random.fold_in(key, 707), (block_count, QUERIES), 0, P_DEV).astype(jnp.int32)
    query_ids = jnp.arange(QUERIES, dtype=jnp.int32)
    word_rows = jnp.broadcast_to((query_ids // 18)[None, :], (block_count, QUERIES))
    bit_values = jnp.broadcast_to(jnp.left_shift(jnp.int32(1), query_ids % 18)[None, :], (block_count, QUERIES))
    point_ids = jnp.arange(block_count, dtype=jnp.int32)[:, None] * P_DEV + chosen
    forced = jnp.zeros((WORDS, NPTS), jnp.int32).at[word_rows, point_ids].max(bit_values)
    return packed | forced


def bell_draw(key, dims, deviation, most, kind=jnp.bfloat16):
    return jnp.clip(deviation * jax.random.normal(key, dims, jnp.float32), -most, most).astype(kind)


def setup_inputs(seed: int = 0) -> dict:
    key_list = jax.random.split(jax.random.key(seed), 13)
    points = draw_points(jax.random.fold_in(key_list[12], 71), 0)
    serial_rank = draw_serial_rank(jax.random.fold_in(key_list[12], 71), 0)
    mask_bits = draw_mask_bits(jax.random.fold_in(key_list[12], 71), 0)
    qkv_weight = draw_qkv_weight(jax.random.fold_in(key_list[12], 71), 0)
    proj_weight = bell_draw(key_list[4], (C, C), C ** -0.5, 0.375)
    up_weight = bell_draw(key_list[5], (C, FF), C ** -0.5, 0.375)
    down_weight = bell_draw(key_list[6], (FF, C), FF ** -0.5, 0.1875)
    queries = draw_queries(jax.random.fold_in(key_list[12], 71), 0)
    dec_q_weight = draw_dec_q_weight(jax.random.fold_in(key_list[12], 71), 0)
    dec_kv_weight = draw_dec_kv_weight(jax.random.fold_in(key_list[12], 71), 0)
    dec_out_weight = bell_draw(key_list[10], (C, C), C ** -0.5, 0.375)
    mask_weight = bell_draw(key_list[11], (C, C), C ** -0.5, 0.375)
    return dict(points=points, serial_rank=serial_rank, mask_bits=mask_bits, qkv_weight=qkv_weight, proj_weight=proj_weight, up_weight=up_weight, down_weight=down_weight, queries=queries, dec_q_weight=dec_q_weight, dec_kv_weight=dec_kv_weight, dec_out_weight=dec_out_weight, mask_weight=mask_weight)


def layer_norm(values):
    average = lax.optimization_barrier(jnp.mean(values, axis=-1, keepdims=True))
    centered = values - average
    variance = lax.optimization_barrier(jnp.mean(centered * centered, axis=-1, keepdims=True))
    return centered * lax.rsqrt(variance + 1e-05)

def patch_attention(patch_rows):
    query_rows = patch_rows[:, :C].reshape(PATCH, HEADS, HDIM).astype(jnp.float32)
    key_rows = patch_rows[:, C:2 * C].reshape(PATCH, HEADS, HDIM).astype(jnp.float32)
    value_rows = patch_rows[:, 2 * C:].reshape(PATCH, HEADS, HDIM).astype(jnp.float32)
    scores = jnp.einsum('qhd,khd->hqk', query_rows, key_rows) * (1.0 / math.sqrt(HDIM))
    weights = lax.optimization_barrier(jax.nn.softmax(scores, axis=-1).astype(jnp.bfloat16)).astype(jnp.float32)
    output = jnp.einsum('hqk,khd->qhd', weights, value_rows)
    return output.reshape(PATCH, C).astype(jnp.bfloat16)

def unpack_bits(words):
    expanded = jnp.repeat(words, 18, axis=0)[:QUERIES]
    shifts = (jnp.arange(QUERIES, dtype=jnp.int32) % 18).astype(jnp.int32)[:, None]
    return jnp.right_shift(expanded, shifts) & 1 == 1

def reference(points, serial_rank, mask_bits, qkv_weight, proj_weight, up_weight, down_weight, queries, dec_q_weight, dec_kv_weight, dec_out_weight, mask_weight):
    normed = layer_norm(points.astype(jnp.float32)).astype(jnp.bfloat16)
    projected = jnp.dot(normed, qkv_weight, preferred_element_type=jnp.float32).astype(jnp.bfloat16)
    grouped = projected.reshape(N_SCENE, GP, 3 * C)
    rolled = jnp.roll(grouped, -(PATCH // 2), axis=1).reshape(NPTS // PATCH, PATCH, 3 * C)
    attended = lax.map(patch_attention, rolled).reshape(N_SCENE, GP, C)
    attended = jnp.roll(attended, PATCH // 2, axis=1).reshape(NPTS, C)
    middle = (points.astype(jnp.float32) + jnp.dot(attended, proj_weight, preferred_element_type=jnp.float32)).astype(jnp.bfloat16)
    normed_mid = layer_norm(middle.astype(jnp.float32)).astype(jnp.bfloat16)
    hidden_units = jax.nn.gelu(jnp.dot(normed_mid, up_weight, preferred_element_type=jnp.float32), approximate=True).astype(jnp.bfloat16)
    block_out = (middle.astype(jnp.float32) + jnp.dot(hidden_units, down_weight, preferred_element_type=jnp.float32)).astype(jnp.bfloat16)
    targets = serial_rank.astype(jnp.int32) + jnp.arange(NPTS, dtype=jnp.int32) // GP * GP
    reserialized = jnp.zeros((NPTS, C), jnp.bfloat16).at[targets].set(block_out)
    point_norm = layer_norm(block_out.astype(jnp.float32)).astype(jnp.bfloat16)
    key_value = jnp.dot(point_norm, dec_kv_weight, preferred_element_type=jnp.float32).astype(jnp.bfloat16)
    query_heads = jnp.dot(queries, dec_q_weight, preferred_element_type=jnp.float32).astype(jnp.bfloat16)
    query_heads = query_heads.reshape(QUERIES, DHEADS, DHDIM).astype(jnp.float32)
    block_count = NPTS // P_DEV
    value_blocks = key_value.reshape(block_count, P_DEV, 2 * C)
    word_blocks = mask_bits.reshape(WORDS, block_count, P_DEV).transpose(1, 0, 2)
    scale = 1.0 / math.sqrt(DHDIM)

    def accumulate(carry, pieces):
        best, total, summed = carry
        rows_block, words_block = pieces
        key_rows = rows_block[:, :C].reshape(P_DEV, DHEADS, DHDIM).astype(jnp.float32)
        value_rows = rows_block[:, C:].reshape(P_DEV, DHEADS, DHDIM).astype(jnp.float32)
        allowed = unpack_bits(words_block)[None, :, :]
        scores = jnp.einsum('qhd,khd->hqk', query_heads, key_rows) * scale
        scores = jnp.where(allowed, scores, jnp.float32(-1e+30))
        new_best = jnp.maximum(best, lax.optimization_barrier(jnp.max(scores, axis=-1)))
        weights = jnp.where(allowed, jnp.exp(scores - new_best[:, :, None]), jnp.float32(0.0))
        factor = jnp.exp(best - new_best)
        total = total * factor + lax.optimization_barrier(jnp.sum(weights, axis=-1))
        summed = summed * factor[:, :, None] + jnp.einsum('hqk,khd->hqd', weights, value_rows, precision=lax.Precision.HIGHEST)
        return ((new_best, total, summed), None)
    start = (jnp.full((DHEADS, QUERIES), -1e+30, jnp.float32), jnp.zeros((DHEADS, QUERIES), jnp.float32), jnp.zeros((DHEADS, QUERIES, DHDIM), jnp.float32))
    (best, total, summed), unused = lax.scan(accumulate, start, (value_blocks, word_blocks))
    cross = (summed / total[:, :, None]).transpose(1, 0, 2).reshape(QUERIES, C).astype(jnp.bfloat16)
    updated = layer_norm(queries.astype(jnp.float32) + jnp.dot(cross, dec_out_weight, preferred_element_type=jnp.float32))
    embed = jnp.dot(updated.astype(jnp.bfloat16), mask_weight, preferred_element_type=jnp.float32).astype(jnp.bfloat16)
    logits = (jnp.dot(embed, point_norm.T, preferred_element_type=jnp.float32) * (1.0 / math.sqrt(C))).astype(jnp.bfloat16)
    return (reserialized, updated, logits)
```

```python
import functools
import math

import jax
import jax.numpy as jnp
from jax import lax
from jax.experimental import pallas as pl
from jax.experimental.pallas import tpu as pltpu
from jax.sharding import PartitionSpec as P

C = 256
HEADS = 16
HDIM = 16
PATCH = 1024
DHEADS = 8
DHDIM = 32
BITS = 18
AUX = 16
STATS = 384
MESH = pl.DeviceIdType.MESH
F32 = jnp.float32
BF16 = jnp.bfloat16


def layer_norm(values):
    average = jnp.mean(values, axis=-1, keepdims=True)
    centered = values - average
    variance = jnp.mean(centered * centered, axis=-1, keepdims=True)
    return centered * lax.rsqrt(variance + 1e-05)


def dot(a, b):
    return jnp.dot(a, b, preferred_element_type=F32)


def dot_t(a, b):
    return lax.dot_general(a, b, (((1,), (1,)), ((), ())), preferred_element_type=F32)


def iota(shape, dim):
    return lax.broadcasted_iota(jnp.int32, shape, dim)


def block_kernel(
    devices,
    x_ref,
    prev_ref,
    next_ref,
    rank_ref,
    qkv_ref,
    proj_ref,
    up_ref,
    down_ref,
    norm_ref,
    out_ref,
    q_s,
    k_s,
    v_s,
    acc_s,
    blk_s,
):
    rows = x_ref.shape[0]
    half = rows // 2
    tile = 256
    ones = jnp.ones((half, 128), BF16)
    normed = layer_norm(x_ref[...].astype(F32)).astype(BF16)
    projected = dot(normed, qkv_ref[...]).astype(BF16)
    for side in range(2):
        own = projected[side * half : (side + 1) * half]
        other_rows = (prev_ref if side == 0 else next_ref)[...]
        other = dot(layer_norm(other_rows.astype(F32)).astype(BF16), qkv_ref[:, C:]).astype(BF16)
        q_s[side] = own[:, :C] * jnp.asarray(1.0 / math.sqrt(HDIM), BF16)
        k_s[side, :half] = own[:, C : 2 * C]
        k_s[side, half:] = other[:, :C]
        for group in range(2):
            lo = 2 * C + 128 * group
            v_s[side, group, :half, :128] = own[:, lo : lo + 128]
            v_s[side, group, :half, 128:] = ones
            v_s[side, group, half:, :128] = other[:, lo - C : lo - C + 128]
            v_s[side, group, half:, 128:] = ones
    acc_s[...] = jnp.zeros_like(acc_s)

    together = (iota((C, C), 0) // HDIM == iota((C, C), 1) // HDIM).astype(BF16)

    def most(ref):
        best = jnp.float32(0.0)
        for side in range(2):
            values = ref[side].astype(F32)
            best = jnp.maximum(best, jnp.max(dot((values * values).astype(BF16), together)))
        return best

    small = most(q_s) * most(k_s) <= 3600.0

    def heads(shifted):
        lane = iota((1, C), 1)

        def step(head, carry):
            for group in range(2):
                q_mask = (lane // HDIM == head + 8 * group).astype(F32).astype(BF16)
                v_mask = ((lane % 128) // HDIM == head).astype(F32).astype(BF16)
                for side in range(2):
                    q = q_s[side] * q_mask
                    total = acc_s[side, group]
                    if shifted:
                        top = jnp.max(dot_t(q, k_s[side]), axis=1, keepdims=True)
                    for start in range(0, 2 * half, tile):
                        scores = dot_t(q, k_s[side, start : start + tile])
                        if shifted:
                            scores = scores - top
                        weights = jnp.exp(scores).astype(BF16)
                        total = total + dot(weights, v_s[side, group, start : start + tile] * v_mask)
                    acc_s[side, group] = total
            return carry

        lax.fori_loop(0, 8, step, 0)

    @pl.when(small)
    def _():
        heads(False)

    @pl.when(jnp.logical_not(small))
    def _():
        heads(True)

    for side in range(2):
        part = slice(side * half, (side + 1) * half)
        attended = jnp.concatenate(
            [acc_s[side, group, :, :128] / acc_s[side, group, :, 128:] for group in range(2)], axis=1
        ).astype(BF16)
        middle = (x_ref[part].astype(F32) + dot(attended, proj_ref[...])).astype(BF16).astype(F32)
        normed_mid = layer_norm(middle).astype(BF16)
        hidden = jax.nn.gelu(dot(normed_mid, up_ref[...]), approximate=True).astype(BF16)
        block = (middle + dot(hidden, down_ref[...])).astype(BF16)
        blk_s[part] = block
        norm_ref[part] = layer_norm(block.astype(F32)).astype(BF16)

    capacity = 2 * rows // devices
    rank = rank_ref[...]
    target = rank // rows
    local = rank % rows
    high = (local // 256 + 1).astype(F32).astype(BF16)
    low = (local % 256).astype(F32).astype(BF16)
    aux_row = iota((AUX, rows), 0)
    aux = jnp.where(aux_row == 0, high.astype(F32), jnp.where(aux_row == 1, low.astype(F32), 0.0)).astype(BF16)
    goes = (iota((devices, rows), 0) == target).astype(F32)
    ahead = (iota((rows, rows), 0) < iota((rows, rows), 1)).astype(F32).astype(BF16)
    before = jnp.sum(goes * dot(goes.astype(BF16), ahead), axis=0, keepdims=True).astype(jnp.int32)
    block = blk_s[...]
    for t in range(devices):
        place = jnp.where(target == t, before, -1)
        chosen = (iota((C, rows), 0) == place).astype(F32).astype(BF16)
        out_ref[t, :capacity] = dot(chosen[:capacity], block).astype(BF16)
        out_ref[t, capacity:] = dot_t(aux, chosen).astype(BF16)


def decoder_kernel(queries_ref, dq_ref, dkv_ref, norm_ref, bits_ref, stats_ref):
    count = queries_ref.shape[0]
    rows = norm_ref.shape[0]
    key_value = dot(norm_ref[...], dkv_ref[...]).astype(BF16)
    query_heads = dot(queries_ref[...], dq_ref[...]).astype(BF16)
    pieces = []
    for start in range(0, count, 8):
        index = iota((8, rows), 0) + start
        first, last = start // BITS, (start + 7) // BITS
        word = bits_ref[first : first + 1, :]
        if last != first:
            word = jnp.where(index < last * BITS, word, bits_ref[last : last + 1, :])
        bit = jnp.right_shift(jnp.broadcast_to(word, (8, rows)), index % BITS) & 1
        pieces.append(jnp.where(bit == 1, 0.0, -1e30).astype(F32))
    bias = jnp.concatenate(pieces, axis=0)
    lane = iota((1, C), 1)
    slot = iota((count, 128), 1)
    stats = jnp.zeros((count, 128), F32)
    for group in range(2):
        total = jnp.zeros((count, C), F32)
        ones = jnp.ones((rows, 128), BF16)
        values = jnp.concatenate([key_value[:, C + 128 * group : C + 128 * (group + 1)], ones], axis=1)
        for inner in range(4):
            head = 4 * group + inner
            q_mask = (lane // DHDIM == head).astype(F32).astype(BF16)
            v_mask = ((lane % 128) // DHDIM == inner).astype(F32).astype(BF16)
            scores = dot_t(query_heads * q_mask, key_value[:, :C]) * (1.0 / math.sqrt(DHDIM)) + bias
            top = jnp.max(scores, axis=1, keepdims=True)
            weights = jnp.exp(scores - top).astype(BF16)
            total = total + dot(weights, values * v_mask)
            stats = jnp.where(slot == head, top, stats)
        for inner in range(4):
            head = 4 * group + inner
            column = 128 + DHDIM * inner
            stats = jnp.where(slot == DHEADS + head, total[:, column : column + 1], stats)
        stats_ref[:count, 128 * group : 128 * (group + 1)] = total[:, :128]
    stats_ref[:count, 2 * 128 :] = stats
    if stats_ref.shape[0] > count:
        rest = stats_ref.shape[0] - count
        stats_ref[count:, :256] = jnp.zeros((rest, 256), F32)
        stats_ref[count:, 256:] = jnp.where(iota((rest, 128), 1) < DHEADS, 0.0, 1.0).astype(F32)


def spread(columns):
    lane = iota((1, C), 1)
    wide = jnp.zeros((columns.shape[0], C), F32)
    for head in range(DHEADS):
        wide = jnp.where(lane // DHDIM == head, columns[:, head : head + 1], wide)
    return wide


def merge(parts):
    best = parts[0][:, C : C + DHEADS]
    for part in parts[1:]:
        best = jnp.maximum(best, part[:, C : C + DHEADS])
    summed, total = 0.0, 0.0
    for part in parts:
        factor = jnp.exp(part[:, C : C + DHEADS] - best)
        summed = summed + part[:, :C] * spread(factor)
        total = total + part[:, C + DHEADS : C + 2 * DHEADS] * factor
    return summed, total, best


def merge_kernel(
    scenes,
    seqs,
    stats_ref,
    queries_ref,
    out_w_ref,
    updated_ref,
    land_a,
    mid,
    land_b,
    result,
    send_a,
    recv_a,
    send_b,
    recv_b,
    send_c,
    recv_c,
    send_d,
    recv_d,
):
    scene, seq = lax.axis_index("scene"), lax.axis_index("seq")
    chunk = stats_ref.shape[0] // scenes
    piece = chunk // seqs

    def on_scene(offset):
        return lax.rem(scene + offset, scenes)

    def on_seq(offset):
        return lax.rem(seq + offset, seqs)

    barrier = pltpu.get_barrier_semaphore()
    for offset in range(1, scenes):
        pl.semaphore_signal(barrier, inc=1, device_id=(on_scene(offset), seq), device_id_type=MESH)
    for offset in range(1, seqs):
        pl.semaphore_signal(barrier, inc=1, device_id=(scene, on_seq(offset)), device_id_type=MESH)
    pl.semaphore_wait(barrier, scenes + seqs - 2)

    def send(source, dest, out_sem, in_sem, device):
        copy = pltpu.make_async_remote_copy(
            src_ref=source, dst_ref=dest, send_sem=out_sem, recv_sem=in_sem,
            device_id=device, device_id_type=MESH,
        )
        copy.start()
        return copy

    copies = []
    for offset in range(1, scenes):
        to = on_scene(offset)
        start = pl.multiple_of(to * chunk, 8)
        copies.append(send(stats_ref.at[pl.ds(start, chunk)], land_a.at[offset - 1],
                           send_a.at[offset - 1], recv_a.at[offset - 1], (to, seq)))
    for copy in copies:
        copy.wait()
    mine = stats_ref[pl.ds(pl.multiple_of(scene * chunk, 8), chunk), :]
    summed, total, best = merge([mine] + [land_a[i] for i in range(scenes - 1)])
    lane = iota((chunk, 128), 1)
    stats = jnp.zeros((chunk, 128), F32)
    for head in range(DHEADS):
        stats = jnp.where(lane == head, best[:, head : head + 1], stats)
        stats = jnp.where(lane == DHEADS + head, total[:, head : head + 1], stats)
    mid[:, :C] = summed
    mid[:, C:] = stats
    copies = []
    for offset in range(1, seqs):
        to = on_seq(offset)
        start = pl.multiple_of(to * piece, 8)
        copies.append(send(mid.at[pl.ds(start, piece)], land_b.at[offset - 1],
                           send_b.at[offset - 1], recv_b.at[offset - 1], (scene, to)))
    for copy in copies:
        copy.wait()
    mine = mid[pl.ds(pl.multiple_of(seq * piece, 8), piece), :]
    summed, total, best = merge([mine] + [land_b[i] for i in range(seqs - 1)])
    cross = (summed / spread(total)).astype(BF16)
    place = pl.multiple_of(scene * chunk + seq * piece, 8)
    rows = queries_ref[pl.ds(place, piece), :] + dot(cross, out_w_ref[...])
    result[pl.ds(place, piece), :] = layer_norm(rows)
    copies = []
    for offset in range(1, seqs):
        part = result.at[pl.ds(place, piece)]
        copies.append(send(part, part, send_c.at[offset - 1], recv_c.at[offset - 1], (scene, on_seq(offset))))
    for copy in copies:
        copy.wait()
    copies = []
    for offset in range(1, scenes):
        part = result.at[pl.ds(pl.multiple_of(scene * chunk, 8), chunk)]
        copies.append(send(part, part, send_d.at[offset - 1], recv_d.at[offset - 1], (on_scene(offset), seq)))
    for copy in copies:
        copy.wait()
    updated_ref[...] = result[...]


def logits_kernel(updated_ref, mask_ref, norm_ref, out_ref):
    embed = dot(updated_ref[...].astype(BF16), mask_ref[...]).astype(BF16)
    out_ref[...] = (dot_t(embed, norm_ref[...]) * (1.0 / math.sqrt(C))).astype(BF16)


def unpack_kernel(devices, in_ref, out_ref):
    rows = out_ref.shape[0]
    capacity = 2 * rows // devices
    total = jnp.zeros(out_ref.shape, F32)
    for t in range(devices):
        aux = in_ref[t, capacity:].astype(F32).astype(jnp.int32)
        slot = (aux[0:1] - 1) * 256 + aux[1:2]
        chosen = (iota((rows, C), 0) == slot).astype(F32).astype(BF16)
        total = total + dot(chosen[:, :capacity], in_ref[t, :capacity])
    out_ref[...] = total.astype(BF16)


def vmem(n):
    return [pl.BlockSpec(memory_space=pltpu.VMEM)] * n


def body(
    points,
    serial_rank,
    mask_bits,
    qkv_weight,
    proj_weight,
    up_weight,
    down_weight,
    queries,
    dec_q_weight,
    dec_kv_weight,
    dec_out_weight,
    mask_weight,
):
    rows = points.shape[0]
    half = rows // 2
    seqs, scenes = lax.axis_size("seq"), lax.axis_size("scene")
    capacity = 2 * rows // seqs
    count = queries.shape[0]
    params = pltpu.CompilerParams(vmem_limit_bytes=56 * 1024 * 1024)
    prev_half = lax.ppermute(points[half:], "seq", [(i, (i + 1) % seqs) for i in range(seqs)])
    next_half = lax.ppermute(points[:half], "seq", [((i + 1) % seqs, i) for i in range(seqs)])
    normed, outgoing = pl.pallas_call(
        functools.partial(block_kernel, seqs),
        out_shape=(
            jax.ShapeDtypeStruct((rows, C), BF16),
            jax.ShapeDtypeStruct((seqs, capacity + AUX, C), BF16),
        ),
        in_specs=vmem(8),
        out_specs=tuple(vmem(2)),
        scratch_shapes=[
            pltpu.VMEM((2, half, C), BF16),
            pltpu.VMEM((2, 2 * half, C), BF16),
            pltpu.VMEM((2, 2, 2 * half, C), BF16),
            pltpu.VMEM((2, 2, half, C), F32),
            pltpu.VMEM((rows, C), BF16),
        ],
        compiler_params=params,
        name="block",
    )(points, prev_half, next_half, serial_rank.reshape(1, rows), qkv_weight, proj_weight, up_weight, down_weight)
    arrived = lax.all_to_all(outgoing, "seq", split_axis=0, concat_axis=0, tiled=True)
    piece = -(-count // (8 * seqs * scenes)) * 8
    padded = piece * seqs * scenes
    stats = pl.pallas_call(
        decoder_kernel,
        out_shape=jax.ShapeDtypeStruct((padded, STATS), F32),
        in_specs=vmem(5),
        out_specs=vmem(1)[0],
        compiler_params=params,
        cost_estimate=pl.CostEstimate(flops=2 * 10**9, bytes_accessed=2 * 10**6, transcendentals=2 * 10**6),
        name="decode",
    )(queries, dec_q_weight, dec_kv_weight, normed, mask_bits)
    wide_queries = jnp.pad(queries.astype(F32), ((0, padded - count), (0, 0)))
    updated = pl.pallas_call(
        functools.partial(merge_kernel, scenes, seqs),
        out_shape=jax.ShapeDtypeStruct((padded, C), F32),
        in_specs=vmem(3),
        out_specs=vmem(1)[0],
        scratch_shapes=[
            pltpu.VMEM((scenes - 1, padded // scenes, STATS), F32),
            pltpu.VMEM((padded // scenes, STATS), F32),
            pltpu.VMEM((seqs - 1, piece, STATS), F32),
            pltpu.VMEM((padded, C), F32),
        ]
        + [pltpu.SemaphoreType.DMA((n - 1,)) for n in (scenes, scenes, seqs, seqs, seqs, seqs, scenes, scenes)],
        compiler_params=pltpu.CompilerParams(collective_id=0, has_side_effects=True),
        cost_estimate=pl.CostEstimate(flops=10**9, bytes_accessed=2 * 10**6, transcendentals=10**5),
        name="merge",
    )(stats, wide_queries, dec_out_weight)
    updated = updated[:count]
    logits = pl.pallas_call(
        logits_kernel,
        out_shape=jax.ShapeDtypeStruct((count, rows), BF16),
        in_specs=vmem(3),
        out_specs=vmem(1)[0],
        compiler_params=params,
        name="logits",
    )(updated, mask_weight, normed)
    reserialized = pl.pallas_call(
        functools.partial(unpack_kernel, seqs),
        out_shape=jax.ShapeDtypeStruct((rows, C), BF16),
        in_specs=vmem(1),
        out_specs=vmem(1)[0],
        compiler_params=params,
        name="unpack",
    )(arrived)
    return (reserialized, updated, logits)


def solution(mesh):
    split = ("scene", "seq")
    in_specs = (P(split, None), P(split), P(None, split)) + (P(),) * 9
    out_specs = (P(split, None), P(), P(None, split))
    return jax.shard_map(body, mesh=mesh, in_specs=in_specs, out_specs=out_specs, check_vma=False)
```

```python
import functools
import math

import jax
import jax.numpy as jnp
from jax import lax
from jax.experimental import pallas as pl
from jax.experimental.pallas import tpu as pltpu
from jax.sharding import PartitionSpec as P

C = 256
HEADS = 16
HDIM = 16
PATCH = 1024
DHEADS = 8
DHDIM = 32
BITS = 18
AUX = 16
STATS = 384
MESH = pl.DeviceIdType.MESH
F32 = jnp.float32
BF16 = jnp.bfloat16


def layer_norm(values):
    average = jnp.mean(values, axis=-1, keepdims=True)
    centered = values - average
    variance = jnp.mean(centered * centered, axis=-1, keepdims=True)
    return centered * lax.rsqrt(variance + 1e-05)


def dot(a, b):
    return jnp.dot(a, b, preferred_element_type=F32)


def dot_t(a, b):
    return lax.dot_general(a, b, (((1,), (1,)), ((), ())), preferred_element_type=F32)


def iota(shape, dim):
    return lax.broadcasted_iota(jnp.int32, shape, dim)


def block_kernel(
    devices,
    x_ref,
    prev_ref,
    next_ref,
    rank_ref,
    qkv_ref,
    proj_ref,
    up_ref,
    down_ref,
    norm_ref,
    out_ref,
    q_s,
    k_s,
    v_s,
    acc_s,
    blk_s,
):
    rows = x_ref.shape[0]
    half = rows // 2
    tile = 256
    ones = jnp.ones((half, 128), BF16)
    normed = layer_norm(x_ref[...].astype(F32)).astype(BF16)
    projected = dot(normed, qkv_ref[...]).astype(BF16)
    for side in range(2):
        own = projected[side * half : (side + 1) * half]
        other_rows = (prev_ref if side == 0 else next_ref)[...]
        other = dot(layer_norm(other_rows.astype(F32)).astype(BF16), qkv_ref[:, C:]).astype(BF16)
        q_s[side] = own[:, :C] * jnp.asarray(1.0 / math.sqrt(HDIM), BF16)
        k_s[side, :half] = own[:, C : 2 * C]
        k_s[side, half:] = other[:, :C]
        for group in range(2):
            lo = 2 * C + 128 * group
            v_s[side, group, :half, :128] = own[:, lo : lo + 128]
            v_s[side, group, :half, 128:] = ones
            v_s[side, group, half:, :128] = other[:, lo - C : lo - C + 128]
            v_s[side, group, half:, 128:] = ones
    acc_s[...] = jnp.zeros_like(acc_s)

    together = (iota((C, C), 0) // HDIM == iota((C, C), 1) // HDIM).astype(BF16)

    def most(ref):
        best = jnp.float32(0.0)
        for side in range(2):
            values = ref[side].astype(F32)
            best = jnp.maximum(best, jnp.max(dot((values * values).astype(BF16), together)))
        return best

    small = most(q_s) * most(k_s) <= 3600.0

    def heads(shifted):
        lane = iota((1, C), 1)

        def step(head, carry):
            for group in range(2):
                q_mask = (lane // HDIM == head + 8 * group).astype(F32).astype(BF16)
                v_mask = ((lane % 128) // HDIM == head).astype(F32).astype(BF16)
                for side in range(2):
                    q = q_s[side] * q_mask
                    total = acc_s[side, group]
                    if shifted:
                        top = jnp.max(dot_t(q, k_s[side]), axis=1, keepdims=True)
                    for start in range(0, 2 * half, tile):
                        scores = dot_t(q, k_s[side, start : start + tile])
                        if shifted:
                            scores = scores - top
                        weights = jnp.exp(scores).astype(BF16)
                        total = total + dot(weights, v_s[side, group, start : start + tile] * v_mask)
                    acc_s[side, group] = total
            return carry

        lax.fori_loop(0, 8, step, 0)

    @pl.when(small)
    def _():
        heads(False)

    @pl.when(jnp.logical_not(small))
    def _():
        heads(True)

    for side in range(2):
        part = slice(side * half, (side + 1) * half)
        attended = jnp.concatenate(
            [acc_s[side, group, :, :128] / acc_s[side, group, :, 128:] for group in range(2)], axis=1
        ).astype(BF16)
        middle = (x_ref[part].astype(F32) + dot(attended, proj_ref[...])).astype(BF16).astype(F32)
        normed_mid = layer_norm(middle).astype(BF16)
        hidden = jax.nn.gelu(dot(normed_mid, up_ref[...]), approximate=True).astype(BF16)
        block = (middle + dot(hidden, down_ref[...])).astype(BF16)
        blk_s[part] = block
        norm_ref[part] = layer_norm(block.astype(F32)).astype(BF16)

    capacity = 2 * rows // devices
    rank = rank_ref[...]
    target = rank // rows
    local = rank % rows
    high = (local // 256 + 1).astype(F32).astype(BF16)
    low = (local % 256).astype(F32).astype(BF16)
    aux_row = iota((AUX, rows), 0)
    aux = jnp.where(aux_row == 0, high.astype(F32), jnp.where(aux_row == 1, low.astype(F32), 0.0)).astype(BF16)
    goes = (iota((devices, rows), 0) == target).astype(F32)
    ahead = (iota((rows, rows), 0) < iota((rows, rows), 1)).astype(F32).astype(BF16)
    before = jnp.sum(goes * dot(goes.astype(BF16), ahead), axis=0, keepdims=True).astype(jnp.int32)
    block = blk_s[...]
    for t in range(devices):
        place = jnp.where(target == t, before, -1)
        chosen = (iota((C, rows), 0) == place).astype(F32).astype(BF16)
        out_ref[t, :capacity] = dot(chosen[:capacity], block).astype(BF16)
        out_ref[t, capacity:] = dot_t(aux, chosen).astype(BF16)


def decoder_kernel(queries_ref, dq_ref, dkv_ref, norm_ref, bits_ref, stats_ref):
    count = queries_ref.shape[0]
    rows = norm_ref.shape[0]
    key_value = dot(norm_ref[...], dkv_ref[...]).astype(BF16)
    query_heads = dot(queries_ref[...], dq_ref[...]).astype(BF16)
    pieces = []
    for start in range(0, count, 8):
        index = iota((8, rows), 0) + start
        first, last = start // BITS, (start + 7) // BITS
        word = bits_ref[first : first + 1, :]
        if last != first:
            word = jnp.where(index < last * BITS, word, bits_ref[last : last + 1, :])
        bit = jnp.right_shift(jnp.broadcast_to(word, (8, rows)), index % BITS) & 1
        pieces.append(jnp.where(bit == 1, 0.0, -1e30).astype(F32))
    bias = jnp.concatenate(pieces, axis=0)
    lane = iota((1, C), 1)
    slot = iota((count, 128), 1)
    stats = jnp.zeros((count, 128), F32)
    for group in range(2):
        total = jnp.zeros((count, C), F32)
        ones = jnp.ones((rows, 128), BF16)
        values = jnp.concatenate([key_value[:, C + 128 * group : C + 128 * (group + 1)], ones], axis=1)
        for inner in range(4):
            head = 4 * group + inner
            q_mask = (lane // DHDIM == head).astype(F32).astype(BF16)
            v_mask = ((lane % 128) // DHDIM == inner).astype(F32).astype(BF16)
            scores = dot_t(query_heads * q_mask, key_value[:, :C]) * (1.0 / math.sqrt(DHDIM)) + bias
            top = jnp.max(scores, axis=1, keepdims=True)
            weights = jnp.exp(scores - top).astype(BF16)
            total = total + dot(weights, values * v_mask)
            stats = jnp.where(slot == head, top, stats)
        for inner in range(4):
            head = 4 * group + inner
            column = 128 + DHDIM * inner
            stats = jnp.where(slot == DHEADS + head, total[:, column : column + 1], stats)
        stats_ref[:count, 128 * group : 128 * (group + 1)] = total[:, :128]
    stats_ref[:count, 2 * 128 :] = stats
    if stats_ref.shape[0] > count:
        rest = stats_ref.shape[0] - count
        stats_ref[count:, :256] = jnp.zeros((rest, 256), F32)
        stats_ref[count:, 256:] = jnp.where(iota((rest, 128), 1) < DHEADS, 0.0, 1.0).astype(F32)


def spread(columns):
    lane = iota((1, C), 1)
    wide = jnp.zeros((columns.shape[0], C), F32)
    for head in range(DHEADS):
        wide = jnp.where(lane // DHDIM == head, columns[:, head : head + 1], wide)
    return wide


def merge(parts):
    best = parts[0][:, C : C + DHEADS]
    for part in parts[1:]:
        best = jnp.maximum(best, part[:, C : C + DHEADS])
    summed, total = 0.0, 0.0
    for part in parts:
        factor = jnp.exp(part[:, C : C + DHEADS] - best)
        summed = summed + part[:, :C] * spread(factor)
        total = total + part[:, C + DHEADS : C + 2 * DHEADS] * factor
    return summed, total, best


def unpack(piece, rows, capacity):
    aux = piece[capacity:].astype(F32).astype(jnp.int32)
    slot = (aux[0:1] - 1) * 256 + aux[1:2]
    chosen = (iota((rows, C), 0) == slot).astype(F32).astype(BF16)
    return dot(chosen[:, :capacity], piece[:capacity])


def tail_kernel(
    scenes,
    seqs,
    outgoing_ref,
    norm_ref,
    bits_ref,
    queries_ref,
    dq_ref,
    dkv_ref,
    out_w_ref,
    mask_ref,
    reserialized_ref,
    updated_ref,
    logits_ref,
    stats_ref,
    wide_ref,
    arrived,
    placed,
    land_a,
    mid,
    land_b,
    result,
    send_a,
    recv_a,
    send_b,
    recv_b,
    send_c,
    recv_c,
    send_d,
    recv_d,
    send_e,
    recv_e,
):
    scene, seq = lax.axis_index("scene"), lax.axis_index("seq")
    count = queries_ref.shape[0]
    rows = norm_ref.shape[0]
    capacity = 2 * rows // seqs
    chunk = stats_ref.shape[0] // scenes
    piece = chunk // seqs

    def on_scene(offset):
        return lax.rem(scene + offset, scenes)

    def on_seq(offset):
        return lax.rem(seq + offset, seqs)

    barrier = pltpu.get_barrier_semaphore()
    for offset in range(1, scenes):
        pl.semaphore_signal(barrier, inc=1, device_id=(on_scene(offset), seq), device_id_type=MESH)
    for offset in range(1, seqs):
        pl.semaphore_signal(barrier, inc=1, device_id=(scene, on_seq(offset)), device_id_type=MESH)
    pl.semaphore_wait(barrier, scenes + seqs - 2)

    def send(source, dest, out_sem, in_sem, device):
        copy = pltpu.make_async_remote_copy(
            src_ref=source, dst_ref=dest, send_sem=out_sem, recv_sem=in_sem,
            device_id=device, device_id_type=MESH,
        )
        copy.start()
        return copy

    order = sorted(range(1, seqs), key=lambda offset: (abs(offset - seqs // 2), offset))
    first, second = len(order) * 4 // 7, len(order) * 6 // 7
    points = []

    def send_points(offsets):
        for offset in offsets:
            to = on_seq(offset)
            copy = send(outgoing_ref.at[to], arrived.at[offset - 1],
                        send_e.at[offset - 1], recv_e.at[offset - 1], (scene, to))
            points.append((offset, copy))

    send_points(order[:first])
    decoder_kernel(queries_ref, dq_ref, dkv_ref, norm_ref, bits_ref, stats_ref)
    wide_ref[:count] = queries_ref[...].astype(F32)
    if wide_ref.shape[0] > count:
        wide_ref[count:] = jnp.zeros((wide_ref.shape[0] - count, C), F32)
    copies = []
    for offset in range(1, scenes):
        to = on_scene(offset)
        start = pl.multiple_of(to * chunk, 8)
        copies.append(send(stats_ref.at[pl.ds(start, chunk)], land_a.at[offset - 1],
                           send_a.at[offset - 1], recv_a.at[offset - 1], (to, seq)))
    placed[...] = unpack(outgoing_ref[seq], rows, capacity)
    for copy in copies:
        copy.wait()
    mine = stats_ref[pl.ds(pl.multiple_of(scene * chunk, 8), chunk), :]
    summed, total, best = merge([mine] + [land_a[i] for i in range(scenes - 1)])
    lane = iota((chunk, 128), 1)
    stats = jnp.zeros((chunk, 128), F32)
    for head in range(DHEADS):
        stats = jnp.where(lane == head, best[:, head : head + 1], stats)
        stats = jnp.where(lane == DHEADS + head, total[:, head : head + 1], stats)
    mid[:, :C] = summed
    mid[:, C:] = stats
    copies = []
    for offset in range(1, seqs):
        to = on_seq(offset)
        start = pl.multiple_of(to * piece, 8)
        copies.append(send(mid.at[pl.ds(start, piece)], land_b.at[offset - 1],
                           send_b.at[offset - 1], recv_b.at[offset - 1], (scene, to)))
    send_points(order[first:second])
    for copy in copies:
        copy.wait()
    mine = mid[pl.ds(pl.multiple_of(seq * piece, 8), piece), :]
    summed, total, best = merge([mine] + [land_b[i] for i in range(seqs - 1)])
    cross = (summed / spread(total)).astype(BF16)
    place = pl.multiple_of(scene * chunk + seq * piece, 8)
    result[pl.ds(place, piece), :] = layer_norm(wide_ref[pl.ds(place, piece), :] + dot(cross, out_w_ref[...]))
    copies = []
    for offset in range(1, seqs):
        part = result.at[pl.ds(place, piece)]
        copies.append(send(part, part, send_c.at[offset - 1], recv_c.at[offset - 1], (scene, on_seq(offset))))
    send_points(order[second:])
    for copy in copies:
        copy.wait()
    copies = []
    for offset in range(1, scenes):
        part = result.at[pl.ds(pl.multiple_of(scene * chunk, 8), chunk)]
        copies.append(send(part, part, send_d.at[offset - 1], recv_d.at[offset - 1], (on_scene(offset), seq)))
    for offset, copy in points[:first]:
        copy.wait()
        placed[...] += unpack(arrived[offset - 1], rows, capacity)
    for copy in copies:
        copy.wait()
    updated = result[:count]
    updated_ref[...] = updated
    embed = dot(updated.astype(BF16), mask_ref[...]).astype(BF16)
    logits_ref[...] = (dot_t(embed, norm_ref[...]) * (1.0 / math.sqrt(C))).astype(BF16)
    for offset, copy in points[first:-1]:
        copy.wait()
        placed[...] += unpack(arrived[offset - 1], rows, capacity)
    offset, copy = points[-1]
    copy.wait()
    reserialized_ref[...] = (placed[...] + unpack(arrived[offset - 1], rows, capacity)).astype(BF16)


def vmem(n):
    return [pl.BlockSpec(memory_space=pltpu.VMEM)] * n


def body(
    points,
    serial_rank,
    mask_bits,
    qkv_weight,
    proj_weight,
    up_weight,
    down_weight,
    queries,
    dec_q_weight,
    dec_kv_weight,
    dec_out_weight,
    mask_weight,
):
    rows = points.shape[0]
    half = rows // 2
    seqs, scenes = lax.axis_size("seq"), lax.axis_size("scene")
    capacity = 2 * rows // seqs
    count = queries.shape[0]
    params = pltpu.CompilerParams(vmem_limit_bytes=56 * 1024 * 1024)
    prev_half = lax.ppermute(points[half:], "seq", [(i, (i + 1) % seqs) for i in range(seqs)])
    next_half = lax.ppermute(points[:half], "seq", [((i + 1) % seqs, i) for i in range(seqs)])
    normed, outgoing = pl.pallas_call(
        functools.partial(block_kernel, seqs),
        out_shape=(
            jax.ShapeDtypeStruct((rows, C), BF16),
            jax.ShapeDtypeStruct((seqs, capacity + AUX, C), BF16),
        ),
        in_specs=vmem(8),
        out_specs=tuple(vmem(2)),
        scratch_shapes=[
            pltpu.VMEM((2, half, C), BF16),
            pltpu.VMEM((2, 2 * half, C), BF16),
            pltpu.VMEM((2, 2, 2 * half, C), BF16),
            pltpu.VMEM((2, 2, half, C), F32),
            pltpu.VMEM((rows, C), BF16),
        ],
        compiler_params=params,
        name="block",
    )(points, prev_half, next_half, serial_rank.reshape(1, rows), qkv_weight, proj_weight, up_weight, down_weight)
    piece = -(-count // (8 * seqs * scenes)) * 8
    padded = piece * seqs * scenes
    return pl.pallas_call(
        functools.partial(tail_kernel, scenes, seqs),
        out_shape=(
            jax.ShapeDtypeStruct((rows, C), BF16),
            jax.ShapeDtypeStruct((count, C), F32),
            jax.ShapeDtypeStruct((count, rows), BF16),
        ),
        in_specs=vmem(8),
        out_specs=tuple(vmem(3)),
        scratch_shapes=[
            pltpu.VMEM((padded, STATS), F32),
            pltpu.VMEM((padded, C), F32),
            pltpu.VMEM((seqs - 1, capacity + AUX, C), BF16),
            pltpu.VMEM((rows, C), F32),
            pltpu.VMEM((scenes - 1, padded // scenes, STATS), F32),
            pltpu.VMEM((padded // scenes, STATS), F32),
            pltpu.VMEM((seqs - 1, piece, STATS), F32),
            pltpu.VMEM((padded, C), F32),
        ]
        + [
            pltpu.SemaphoreType.DMA((n - 1,))
            for n in (scenes, scenes, seqs, seqs, seqs, seqs, scenes, scenes, seqs, seqs)
        ],
        compiler_params=pltpu.CompilerParams(
            collective_id=0, has_side_effects=True, vmem_limit_bytes=56 * 1024 * 1024
        ),
        name="tail",
    )(outgoing, normed, mask_bits, queries, dec_q_weight, dec_kv_weight, dec_out_weight, mask_weight)


def solution(mesh):
    split = ("scene", "seq")
    in_specs = (P(split, None), P(split), P(None, split)) + (P(),) * 9
    out_specs = (P(split, None), P(), P(None, split))
    return jax.shard_map(body, mesh=mesh, in_specs=in_specs, out_specs=out_specs, check_vma=False)
```

```python
import functools
import math

import jax
import jax.numpy as jnp
from jax import lax
from jax.experimental import pallas as pl
from jax.experimental.pallas import tpu as pltpu
from jax.sharding import PartitionSpec as P

C = 256
HEADS = 16
HDIM = 16
PATCH = 1024
DHEADS = 8
DHDIM = 32
BITS = 18
AUX = 16
STATS = 384
MESH = pl.DeviceIdType.MESH
F32 = jnp.float32
BF16 = jnp.bfloat16


def layer_norm(values):
    average = jnp.mean(values, axis=-1, keepdims=True)
    centered = values - average
    variance = jnp.mean(centered * centered, axis=-1, keepdims=True)
    return centered * lax.rsqrt(variance + 1e-05)


def dot(a, b):
    return jnp.dot(a, b, preferred_element_type=F32)


def dot_t(a, b):
    return lax.dot_general(a, b, (((1,), (1,)), ((), ())), preferred_element_type=F32)


def iota(shape, dim):
    return lax.broadcasted_iota(jnp.int32, shape, dim)


def group_masks(head, group):
    lane = iota((1, C), 1)
    q_mask = (lane // HDIM == head + 8 * group).astype(F32).astype(BF16)
    v_mask = ((lane % 128) // HDIM == head).astype(F32)
    return q_mask, v_mask


def fill(side, key_value, k_s, v_s):
    k_s[side] = key_value[:, :C]
    for group in range(2):
        v_s[side, group, :, :128] = key_value[:, C + 128 * group : C + 128 * (group + 1)]
        v_s[side, group, :, 128:] = jnp.ones((key_value.shape[0], 128), BF16)


def most(ref):
    together = (iota((C, C), 0) // HDIM == iota((C, C), 1) // HDIM).astype(BF16)
    best = jnp.float32(0.0)
    for side in range(2):
        values = ref[side].astype(F32)
        best = jnp.maximum(best, jnp.max(dot((values * values).astype(BF16), together)))
    return best


def attend(q_ref, k_s, v_s, acc_s, shift):
    keys = k_s.shape[1]
    tile = 256

    def step(head, carry):
        for group in range(2):
            q_mask, v_mask = group_masks(head, group)
            v_mask = v_mask.astype(BF16)
            for side in range(2):
                q = q_ref[side] * q_mask
                total = acc_s[side, group]
                if shift is not None:
                    top = shift(side, group, head, jnp.max(dot_t(q, k_s[side]), axis=1, keepdims=True))
                for start in range(0, keys, tile):
                    scores = dot_t(q, k_s[side, start : start + tile])
                    if shift is not None:
                        scores = scores - top
                    weights = jnp.exp(scores).astype(BF16)
                    total = total + dot(weights, v_s[side, group, start : start + tile] * v_mask)
                acc_s[side, group] = total
        return carry

    lax.fori_loop(0, 8, step, 0)


def own_kernel(x_ref, qkv_ref, q_ref, acc_ref, top_ref, flag_ref, k_s, v_s):
    half = x_ref.shape[0] // 2
    normed = layer_norm(x_ref[...].astype(F32)).astype(BF16)
    projected = dot(normed, qkv_ref[...]).astype(BF16)
    for side in range(2):
        own = projected[side * half : (side + 1) * half]
        q_ref[side] = own[:, :C] * jnp.asarray(1.0 / math.sqrt(HDIM), BF16)
        fill(side, own[:, C:], k_s, v_s)
    acc_ref[...] = jnp.zeros_like(acc_ref)
    top_ref[...] = jnp.zeros_like(top_ref)
    most_q = most(q_ref)
    small = most_q * most(k_s) <= 3600.0
    flag_ref[0] = most_q
    flag_ref[1] = jnp.where(small, 1.0, 0.0)

    def shift(side, group, head, peak):
        lane = iota((1, 128), 1)
        top_ref[side] = jnp.where(lane == head + 8 * group, peak, top_ref[side])
        return peak

    @pl.when(small)
    def _():
        attend(q_ref, k_s, v_s, acc_ref, None)

    @pl.when(jnp.logical_not(small))
    def _():
        attend(q_ref, k_s, v_s, acc_ref, shift)


def block_kernel(
    devices,
    x_ref,
    prev_ref,
    next_ref,
    rank_ref,
    qkv_ref,
    proj_ref,
    up_ref,
    down_ref,
    q_ref,
    old_ref,
    top_ref,
    flag_ref,
    norm_ref,
    out_ref,
    k_s,
    v_s,
    acc_s,
    scale_s,
    blk_s,
):
    rows = x_ref.shape[0]
    half = rows // 2
    for side in range(2):
        other_rows = (prev_ref if side == 0 else next_ref)[...]
        other = dot(layer_norm(other_rows.astype(F32)).astype(BF16), qkv_ref[:, C:]).astype(BF16)
        fill(side, other, k_s, v_s)
    small = jnp.logical_and(flag_ref[0] * most(k_s) <= 3600.0, flag_ref[1] > 0.5)

    def shift(side, group, head, peak):
        lane = iota((1, 128), 1)
        old = jnp.max(jnp.where(lane == head + 8 * group, top_ref[side], -jnp.inf), axis=1, keepdims=True)
        top = jnp.maximum(old, peak)
        mask = group_masks(head, group)[1]
        scale_s[side, group] = jnp.where(mask > 0.5, jnp.exp(old - top), scale_s[side, group])
        return top

    @pl.when(small)
    def _():
        acc_s[...] = old_ref[...]
        attend(q_ref, k_s, v_s, acc_s, None)

    @pl.when(jnp.logical_not(small))
    def _():
        acc_s[...] = jnp.zeros_like(acc_s)
        attend(q_ref, k_s, v_s, acc_s, shift)
        acc_s[...] = acc_s[...] + old_ref[...] * scale_s[...]

    for side in range(2):
        part = slice(side * half, (side + 1) * half)
        attended = jnp.concatenate(
            [acc_s[side, group, :, :128] / acc_s[side, group, :, 128:] for group in range(2)], axis=1
        ).astype(BF16)
        middle = (x_ref[part].astype(F32) + dot(attended, proj_ref[...])).astype(BF16).astype(F32)
        normed_mid = layer_norm(middle).astype(BF16)
        hidden = jax.nn.gelu(dot(normed_mid, up_ref[...]), approximate=True).astype(BF16)
        block = (middle + dot(hidden, down_ref[...])).astype(BF16)
        blk_s[part] = block
        norm_ref[part] = layer_norm(block.astype(F32)).astype(BF16)

    capacity = 2 * rows // devices
    rank = rank_ref[...]
    target = rank // rows
    local = rank % rows
    high = (local // 256 + 1).astype(F32).astype(BF16)
    low = (local % 256).astype(F32).astype(BF16)
    aux_row = iota((AUX, rows), 0)
    aux = jnp.where(aux_row == 0, high.astype(F32), jnp.where(aux_row == 1, low.astype(F32), 0.0)).astype(BF16)
    goes = (iota((devices, rows), 0) == target).astype(F32)
    ahead = (iota((rows, rows), 0) < iota((rows, rows), 1)).astype(F32).astype(BF16)
    before = jnp.sum(goes * dot(goes.astype(BF16), ahead), axis=0, keepdims=True).astype(jnp.int32)
    block = blk_s[...]
    for t in range(devices):
        place = jnp.where(target == t, before, -1)
        chosen = (iota((C, rows), 0) == place).astype(F32).astype(BF16)
        out_ref[t, :capacity] = dot(chosen[:capacity], block).astype(BF16)
        out_ref[t, capacity:] = dot_t(aux, chosen).astype(BF16)


def decoder_kernel(queries_ref, dq_ref, dkv_ref, norm_ref, bits_ref, stats_ref):
    count = queries_ref.shape[0]
    rows = norm_ref.shape[0]
    key_value = dot(norm_ref[...], dkv_ref[...]).astype(BF16)
    query_heads = dot(queries_ref[...], dq_ref[...]).astype(BF16)
    pieces = []
    for start in range(0, count, 8):
        index = iota((8, rows), 0) + start
        first, last = start // BITS, (start + 7) // BITS
        word = bits_ref[first : first + 1, :]
        if last != first:
            word = jnp.where(index < last * BITS, word, bits_ref[last : last + 1, :])
        bit = jnp.right_shift(jnp.broadcast_to(word, (8, rows)), index % BITS) & 1
        pieces.append(jnp.where(bit == 1, 0.0, -1e30).astype(F32))
    bias = jnp.concatenate(pieces, axis=0)
    lane = iota((1, C), 1)
    slot = iota((count, 128), 1)
    stats = jnp.zeros((count, 128), F32)
    for group in range(2):
        total = jnp.zeros((count, C), F32)
        ones = jnp.ones((rows, 128), BF16)
        values = jnp.concatenate([key_value[:, C + 128 * group : C + 128 * (group + 1)], ones], axis=1)
        for inner in range(4):
            head = 4 * group + inner
            q_mask = (lane // DHDIM == head).astype(F32).astype(BF16)
            v_mask = ((lane % 128) // DHDIM == inner).astype(F32).astype(BF16)
            scores = dot_t(query_heads * q_mask, key_value[:, :C]) * (1.0 / math.sqrt(DHDIM)) + bias
            top = jnp.max(scores, axis=1, keepdims=True)
            weights = jnp.exp(scores - top).astype(BF16)
            total = total + dot(weights, values * v_mask)
            stats = jnp.where(slot == head, top, stats)
        for inner in range(4):
            head = 4 * group + inner
            column = 128 + DHDIM * inner
            stats = jnp.where(slot == DHEADS + head, total[:, column : column + 1], stats)
        stats_ref[:count, 128 * group : 128 * (group + 1)] = total[:, :128]
    stats_ref[:count, 2 * 128 :] = stats
    if stats_ref.shape[0] > count:
        rest = stats_ref.shape[0] - count
        stats_ref[count:, :256] = jnp.zeros((rest, 256), F32)
        stats_ref[count:, 256:] = jnp.where(iota((rest, 128), 1) < DHEADS, 0.0, 1.0).astype(F32)


def spread(columns):
    lane = iota((1, C), 1)
    wide = jnp.zeros((columns.shape[0], C), F32)
    for head in range(DHEADS):
        wide = jnp.where(lane // DHDIM == head, columns[:, head : head + 1], wide)
    return wide


def merge(parts):
    best = parts[0][:, C : C + DHEADS]
    for part in parts[1:]:
        best = jnp.maximum(best, part[:, C : C + DHEADS])
    summed, total = 0.0, 0.0
    for part in parts:
        factor = jnp.exp(part[:, C : C + DHEADS] - best)
        summed = summed + part[:, :C] * spread(factor)
        total = total + part[:, C + DHEADS : C + 2 * DHEADS] * factor
    return summed, total, best


def unpack(piece, rows, capacity):
    aux = piece[capacity:].astype(F32).astype(jnp.int32)
    slot = (aux[0:1] - 1) * 256 + aux[1:2]
    chosen = (iota((rows, C), 0) == slot).astype(F32).astype(BF16)
    return dot(chosen[:, :capacity], piece[:capacity])


def tail_kernel(
    scenes,
    seqs,
    outgoing_ref,
    norm_ref,
    bits_ref,
    queries_ref,
    dq_ref,
    dkv_ref,
    out_w_ref,
    mask_ref,
    reserialized_ref,
    updated_ref,
    logits_ref,
    stats_ref,
    wide_ref,
    arrived,
    placed,
    land_a,
    mid,
    land_b,
    result,
    send_a,
    recv_a,
    send_b,
    recv_b,
    send_c,
    recv_c,
    send_d,
    recv_d,
    send_e,
    recv_e,
):
    scene, seq = lax.axis_index("scene"), lax.axis_index("seq")
    count = queries_ref.shape[0]
    rows = norm_ref.shape[0]
    capacity = 2 * rows // seqs
    chunk = stats_ref.shape[0] // scenes
    piece = chunk // seqs

    def on_scene(offset):
        return lax.rem(scene + offset, scenes)

    def on_seq(offset):
        return lax.rem(seq + offset, seqs)

    barrier = pltpu.get_barrier_semaphore()
    for offset in range(1, scenes):
        pl.semaphore_signal(barrier, inc=1, device_id=(on_scene(offset), seq), device_id_type=MESH)
    for offset in range(1, seqs):
        pl.semaphore_signal(barrier, inc=1, device_id=(scene, on_seq(offset)), device_id_type=MESH)
    pl.semaphore_wait(barrier, scenes + seqs - 2)

    def send(source, dest, out_sem, in_sem, device):
        copy = pltpu.make_async_remote_copy(
            src_ref=source, dst_ref=dest, send_sem=out_sem, recv_sem=in_sem,
            device_id=device, device_id_type=MESH,
        )
        copy.start()
        return copy

    order = sorted(range(1, seqs), key=lambda offset: (abs(offset - seqs // 2), offset))
    first, second = len(order) * 4 // 7, len(order) * 6 // 7
    points = []

    def send_points(offsets):
        for offset in offsets:
            to = on_seq(offset)
            copy = send(outgoing_ref.at[to], arrived.at[offset - 1],
                        send_e.at[offset - 1], recv_e.at[offset - 1], (scene, to))
            points.append((offset, copy))

    send_points(order[:first])
    decoder_kernel(queries_ref, dq_ref, dkv_ref, norm_ref, bits_ref, stats_ref)
    wide_ref[:count] = queries_ref[...].astype(F32)
    if wide_ref.shape[0] > count:
        wide_ref[count:] = jnp.zeros((wide_ref.shape[0] - count, C), F32)
    copies = []
    for offset in range(1, scenes):
        to = on_scene(offset)
        start = pl.multiple_of(to * chunk, 8)
        copies.append(send(stats_ref.at[pl.ds(start, chunk)], land_a.at[offset - 1],
                           send_a.at[offset - 1], recv_a.at[offset - 1], (to, seq)))
    placed[...] = unpack(outgoing_ref[seq], rows, capacity)
    for copy in copies:
        copy.wait()
    mine = stats_ref[pl.ds(pl.multiple_of(scene * chunk, 8), chunk), :]
    summed, total, best = merge([mine] + [land_a[i] for i in range(scenes - 1)])
    lane = iota((chunk, 128), 1)
    stats = jnp.zeros((chunk, 128), F32)
    for head in range(DHEADS):
        stats = jnp.where(lane == head, best[:, head : head + 1], stats)
        stats = jnp.where(lane == DHEADS + head, total[:, head : head + 1], stats)
    mid[:, :C] = summed
    mid[:, C:] = stats
    copies = []
    for offset in range(1, seqs):
        to = on_seq(offset)
        start = pl.multiple_of(to * piece, 8)
        copies.append(send(mid.at[pl.ds(start, piece)], land_b.at[offset - 1],
                           send_b.at[offset - 1], recv_b.at[offset - 1], (scene, to)))
    send_points(order[first:second])
    for copy in copies:
        copy.wait()
    mine = mid[pl.ds(pl.multiple_of(seq * piece, 8), piece), :]
    summed, total, best = merge([mine] + [land_b[i] for i in range(seqs - 1)])
    cross = (summed / spread(total)).astype(BF16)
    place = pl.multiple_of(scene * chunk + seq * piece, 8)
    result[pl.ds(place, piece), :] = layer_norm(wide_ref[pl.ds(place, piece), :] + dot(cross, out_w_ref[...]))
    copies = []
    for offset in range(1, seqs):
        part = result.at[pl.ds(place, piece)]
        copies.append(send(part, part, send_c.at[offset - 1], recv_c.at[offset - 1], (scene, on_seq(offset))))
    send_points(order[second:])
    for copy in copies:
        copy.wait()
    copies = []
    for offset in range(1, scenes):
        part = result.at[pl.ds(pl.multiple_of(scene * chunk, 8), chunk)]
        copies.append(send(part, part, send_d.at[offset - 1], recv_d.at[offset - 1], (on_scene(offset), seq)))
    for offset, copy in points[:first]:
        copy.wait()
        placed[...] += unpack(arrived[offset - 1], rows, capacity)
    for copy in copies:
        copy.wait()
    updated = result[:count]
    updated_ref[...] = updated
    embed = dot(updated.astype(BF16), mask_ref[...]).astype(BF16)
    logits_ref[...] = (dot_t(embed, norm_ref[...]) * (1.0 / math.sqrt(C))).astype(BF16)
    for offset, copy in points[first:-1]:
        copy.wait()
        placed[...] += unpack(arrived[offset - 1], rows, capacity)
    offset, copy = points[-1]
    copy.wait()
    reserialized_ref[...] = (placed[...] + unpack(arrived[offset - 1], rows, capacity)).astype(BF16)


def vmem(n):
    return [pl.BlockSpec(memory_space=pltpu.VMEM)] * n


def body(
    points,
    serial_rank,
    mask_bits,
    qkv_weight,
    proj_weight,
    up_weight,
    down_weight,
    queries,
    dec_q_weight,
    dec_kv_weight,
    dec_out_weight,
    mask_weight,
):
    rows = points.shape[0]
    half = rows // 2
    seqs, scenes = lax.axis_size("seq"), lax.axis_size("scene")
    capacity = 2 * rows // seqs
    count = queries.shape[0]
    params = pltpu.CompilerParams(vmem_limit_bytes=32 * 1024 * 1024)
    prev_half = lax.ppermute(points[half:], "seq", [(i, (i + 1) % seqs) for i in range(seqs)])
    next_half = lax.ppermute(points[:half], "seq", [((i + 1) % seqs, i) for i in range(seqs)])
    smem = pl.BlockSpec(memory_space=pltpu.SMEM)
    kept = [pltpu.VMEM((2, half, C), BF16), pltpu.VMEM((2, 2, half, C), BF16)]
    own = pl.pallas_call(
        own_kernel,
        out_shape=(
            jax.ShapeDtypeStruct((2, half, C), BF16),
            jax.ShapeDtypeStruct((2, 2, half, C), F32),
            jax.ShapeDtypeStruct((2, half, 128), F32),
            jax.ShapeDtypeStruct((2,), F32),
        ),
        in_specs=vmem(2),
        out_specs=tuple(vmem(3)) + (smem,),
        scratch_shapes=kept,
        compiler_params=params,
        cost_estimate=pl.CostEstimate(flops=10**10, bytes_accessed=4 * 10**6, transcendentals=8 * 10**6),
        name="own",
    )(points, qkv_weight)
    normed, outgoing = pl.pallas_call(
        functools.partial(block_kernel, seqs),
        out_shape=(
            jax.ShapeDtypeStruct((rows, C), BF16),
            jax.ShapeDtypeStruct((seqs, capacity + AUX, C), BF16),
        ),
        in_specs=vmem(11) + [smem],
        out_specs=tuple(vmem(2)),
        scratch_shapes=kept
        + [
            pltpu.VMEM((2, 2, half, C), F32),
            pltpu.VMEM((2, 2, half, C), F32),
            pltpu.VMEM((rows, C), BF16),
        ],
        compiler_params=params,
        name="block",
    )(
        points, prev_half, next_half, serial_rank.reshape(1, rows), qkv_weight, proj_weight, up_weight, down_weight, *own
    )
    piece = -(-count // (8 * seqs * scenes)) * 8
    padded = piece * seqs * scenes
    return pl.pallas_call(
        functools.partial(tail_kernel, scenes, seqs),
        out_shape=(
            jax.ShapeDtypeStruct((rows, C), BF16),
            jax.ShapeDtypeStruct((count, C), F32),
            jax.ShapeDtypeStruct((count, rows), BF16),
        ),
        in_specs=vmem(8),
        out_specs=tuple(vmem(3)),
        scratch_shapes=[
            pltpu.VMEM((padded, STATS), F32),
            pltpu.VMEM((padded, C), F32),
            pltpu.VMEM((seqs - 1, capacity + AUX, C), BF16),
            pltpu.VMEM((rows, C), F32),
            pltpu.VMEM((scenes - 1, padded // scenes, STATS), F32),
            pltpu.VMEM((padded // scenes, STATS), F32),
            pltpu.VMEM((seqs - 1, piece, STATS), F32),
            pltpu.VMEM((padded, C), F32),
        ]
        + [
            pltpu.SemaphoreType.DMA((n - 1,))
            for n in (scenes, scenes, seqs, seqs, seqs, seqs, scenes, scenes, seqs, seqs)
        ],
        compiler_params=pltpu.CompilerParams(
            collective_id=0, has_side_effects=True, vmem_limit_bytes=32 * 1024 * 1024
        ),
        name="tail",
    )(outgoing, normed, mask_bits, queries, dec_q_weight, dec_kv_weight, dec_out_weight, mask_weight)


def solution(mesh):
    split = ("scene", "seq")
    in_specs = (P(split, None), P(split), P(None, split)) + (P(),) * 9
    out_specs = (P(split, None), P(), P(None, split))
    return jax.shard_map(body, mesh=mesh, in_specs=in_specs, out_specs=out_specs, check_vma=False)
```

```python
import functools
import math

import jax
import jax.numpy as jnp
from jax import lax
from jax.experimental import pallas as pl
from jax.experimental.pallas import tpu as pltpu
from jax.sharding import PartitionSpec as P

C = 256
HEADS = 16
HDIM = 16
PATCH = 1024
DHEADS = 8
DHDIM = 32
BITS = 18
AUX = 16
STATS = 384
MESH = pl.DeviceIdType.MESH
F32 = jnp.float32
BF16 = jnp.bfloat16


def layer_norm(values):
    average = jnp.mean(values, axis=-1, keepdims=True)
    centered = values - average
    variance = jnp.mean(centered * centered, axis=-1, keepdims=True)
    return centered * lax.rsqrt(variance + 1e-05)


def dot(a, b):
    return jnp.dot(a, b, preferred_element_type=F32)


def dot_t(a, b):
    return lax.dot_general(a, b, (((1,), (1,)), ((), ())), preferred_element_type=F32)


def iota(shape, dim):
    return lax.broadcasted_iota(jnp.int32, shape, dim)


def group_masks(head, group):
    lane = iota((1, C), 1)
    q_mask = (lane // HDIM == head + 8 * group).astype(F32).astype(BF16)
    v_mask = ((lane % 128) // HDIM == head).astype(F32)
    return q_mask, v_mask


def fill(side, key_value, k_s, v_s):
    k_s[side] = key_value[:, :C]
    for group in range(2):
        v_s[side, group, :, :128] = key_value[:, C + 128 * group : C + 128 * (group + 1)]
        v_s[side, group, :, 128:] = jnp.ones((key_value.shape[0], 128), BF16)


def most(ref):
    together = (iota((C, C), 0) // HDIM == iota((C, C), 1) // HDIM).astype(BF16)
    best = jnp.float32(0.0)
    for side in range(2):
        values = ref[side].astype(F32)
        best = jnp.maximum(best, jnp.max(dot((values * values).astype(BF16), together)))
    return best


def attend(q_ref, k_s, v_s, acc_s, shift):
    keys = k_s.shape[1]
    tile = 512

    def step(head, carry):
        for group in range(2):
            q_mask, v_mask = group_masks(head, group)
            v_mask = v_mask.astype(BF16)
            for side in range(2):
                q = q_ref[side] * q_mask
                total = acc_s[side, group]
                if shift is not None:
                    top = shift(side, group, head, jnp.max(dot_t(q, k_s[side]), axis=1, keepdims=True))
                for start in range(0, keys, tile):
                    scores = dot_t(q, k_s[side, start : start + tile])
                    if shift is not None:
                        scores = scores - top
                    weights = jnp.exp(scores).astype(BF16)
                    total = total + dot(weights, v_s[side, group, start : start + tile] * v_mask)
                acc_s[side, group] = total
        return carry

    lax.fori_loop(0, 8, step, 0)


def own_kernel(x_ref, qkv_ref, q_ref, acc_ref, top_ref, flag_ref, k_s, v_s):
    half = x_ref.shape[0] // 2
    normed = layer_norm(x_ref[...].astype(F32)).astype(BF16)
    projected = dot(normed, qkv_ref[...]).astype(BF16)
    for side in range(2):
        own = projected[side * half : (side + 1) * half]
        q_ref[side] = own[:, :C] * jnp.asarray(1.0 / math.sqrt(HDIM), BF16)
        fill(side, own[:, C:], k_s, v_s)
    acc_ref[...] = jnp.zeros_like(acc_ref)
    top_ref[...] = jnp.zeros_like(top_ref)
    most_q = most(q_ref)
    small = most_q * most(k_s) <= 3600.0
    flag_ref[0] = most_q
    flag_ref[1] = jnp.where(small, 1.0, 0.0)

    def shift(side, group, head, peak):
        lane = iota((1, 128), 1)
        top_ref[side] = jnp.where(lane == head + 8 * group, peak, top_ref[side])
        return peak

    @pl.when(small)
    def _():
        attend(q_ref, k_s, v_s, acc_ref, None)

    @pl.when(jnp.logical_not(small))
    def _():
        attend(q_ref, k_s, v_s, acc_ref, shift)


def block_kernel(
    devices,
    x_ref,
    prev_ref,
    next_ref,
    rank_ref,
    qkv_ref,
    proj_ref,
    up_ref,
    down_ref,
    q_ref,
    old_ref,
    top_ref,
    flag_ref,
    norm_ref,
    out_ref,
    k_s,
    v_s,
    acc_s,
    scale_s,
    blk_s,
):
    rows = x_ref.shape[0]
    half = rows // 2
    for side in range(2):
        other_rows = (prev_ref if side == 0 else next_ref)[...]
        other = dot(layer_norm(other_rows.astype(F32)).astype(BF16), qkv_ref[:, C:]).astype(BF16)
        fill(side, other, k_s, v_s)
    small = jnp.logical_and(flag_ref[0] * most(k_s) <= 3600.0, flag_ref[1] > 0.5)

    def shift(side, group, head, peak):
        lane = iota((1, 128), 1)
        old = jnp.max(jnp.where(lane == head + 8 * group, top_ref[side], -jnp.inf), axis=1, keepdims=True)
        top = jnp.maximum(old, peak)
        mask = group_masks(head, group)[1]
        scale_s[side, group] = jnp.where(mask > 0.5, jnp.exp(old - top), scale_s[side, group])
        return top

    @pl.when(small)
    def _():
        acc_s[...] = old_ref[...]
        attend(q_ref, k_s, v_s, acc_s, None)

    @pl.when(jnp.logical_not(small))
    def _():
        acc_s[...] = jnp.zeros_like(acc_s)
        attend(q_ref, k_s, v_s, acc_s, shift)
        acc_s[...] = acc_s[...] + old_ref[...] * scale_s[...]

    for side in range(2):
        part = slice(side * half, (side + 1) * half)
        attended = jnp.concatenate(
            [acc_s[side, group, :, :128] / acc_s[side, group, :, 128:] for group in range(2)], axis=1
        ).astype(BF16)
        middle = (x_ref[part].astype(F32) + dot(attended, proj_ref[...])).astype(BF16).astype(F32)
        normed_mid = layer_norm(middle).astype(BF16)
        hidden = jax.nn.gelu(dot(normed_mid, up_ref[...]), approximate=True).astype(BF16)
        block = (middle + dot(hidden, down_ref[...])).astype(BF16)
        blk_s[part] = block
        norm_ref[part] = layer_norm(block.astype(F32)).astype(BF16)

    capacity = 2 * rows // devices
    rank = rank_ref[...]
    target = rank // rows
    local = rank % rows
    high = (local // 256 + 1).astype(F32).astype(BF16)
    low = (local % 256).astype(F32).astype(BF16)
    aux_row = iota((AUX, rows), 0)
    aux = jnp.where(aux_row == 0, high.astype(F32), jnp.where(aux_row == 1, low.astype(F32), 0.0)).astype(BF16)
    goes = (iota((devices, rows), 0) == target).astype(F32)
    ahead = (iota((rows, rows), 0) < iota((rows, rows), 1)).astype(F32).astype(BF16)
    before = jnp.sum(goes * dot(goes.astype(BF16), ahead), axis=0, keepdims=True).astype(jnp.int32)
    block = blk_s[...]
    for t in range(devices):
        place = jnp.where(target == t, before, -1)
        chosen = (iota((C, rows), 0) == place).astype(F32).astype(BF16)
        out_ref[t, :capacity] = dot(chosen[:capacity], block).astype(BF16)
        out_ref[t, capacity:] = dot_t(aux, chosen).astype(BF16)


def decoder_kernel(queries_ref, dq_ref, dkv_ref, norm_ref, bits_ref, stats_ref):
    count = queries_ref.shape[0]
    rows = norm_ref.shape[0]
    key_value = dot(norm_ref[...], dkv_ref[...]).astype(BF16)
    query_heads = dot(queries_ref[...], dq_ref[...]).astype(BF16)
    pieces = []
    for start in range(0, count, 8):
        index = iota((8, rows), 0) + start
        first, last = start // BITS, (start + 7) // BITS
        word = bits_ref[first : first + 1, :]
        if last != first:
            word = jnp.where(index < last * BITS, word, bits_ref[last : last + 1, :])
        bit = jnp.right_shift(jnp.broadcast_to(word, (8, rows)), index % BITS) & 1
        pieces.append(jnp.where(bit == 1, 0.0, -1e30).astype(F32))
    bias = jnp.concatenate(pieces, axis=0)
    lane = iota((1, C), 1)
    slot = iota((count, 128), 1)
    stats = jnp.zeros((count, 128), F32)
    for group in range(2):
        total = jnp.zeros((count, C), F32)
        ones = jnp.ones((rows, 128), BF16)
        values = jnp.concatenate([key_value[:, C + 128 * group : C + 128 * (group + 1)], ones], axis=1)
        for inner in range(4):
            head = 4 * group + inner
            q_mask = (lane // DHDIM == head).astype(F32).astype(BF16)
            v_mask = ((lane % 128) // DHDIM == inner).astype(F32).astype(BF16)
            scores = dot_t(query_heads * q_mask, key_value[:, :C]) * (1.0 / math.sqrt(DHDIM)) + bias
            top = jnp.max(scores, axis=1, keepdims=True)
            weights = jnp.exp(scores - top).astype(BF16)
            total = total + dot(weights, values * v_mask)
            stats = jnp.where(slot == head, top, stats)
        for inner in range(4):
            head = 4 * group + inner
            column = 128 + DHDIM * inner
            stats = jnp.where(slot == DHEADS + head, total[:, column : column + 1], stats)
        stats_ref[:count, 128 * group : 128 * (group + 1)] = total[:, :128]
    stats_ref[:count, 2 * 128 :] = stats
    if stats_ref.shape[0] > count:
        rest = stats_ref.shape[0] - count
        stats_ref[count:, :256] = jnp.zeros((rest, 256), F32)
        stats_ref[count:, 256:] = jnp.where(iota((rest, 128), 1) < DHEADS, 0.0, 1.0).astype(F32)


def spread(columns):
    lane = iota((1, C), 1)
    wide = jnp.zeros((columns.shape[0], C), F32)
    for head in range(DHEADS):
        wide = jnp.where(lane // DHDIM == head, columns[:, head : head + 1], wide)
    return wide


def merge(parts):
    best = parts[0][:, C : C + DHEADS]
    for part in parts[1:]:
        best = jnp.maximum(best, part[:, C : C + DHEADS])
    summed, total = 0.0, 0.0
    for part in parts:
        factor = jnp.exp(part[:, C : C + DHEADS] - best)
        summed = summed + part[:, :C] * spread(factor)
        total = total + part[:, C + DHEADS : C + 2 * DHEADS] * factor
    return summed, total, best


def unpack(piece, rows, capacity):
    aux = piece[capacity:].astype(F32).astype(jnp.int32)
    slot = (aux[0:1] - 1) * 256 + aux[1:2]
    chosen = (iota((rows, C), 0) == slot).astype(F32).astype(BF16)
    return dot(chosen[:, :capacity], piece[:capacity])


def tail_kernel(
    scenes,
    seqs,
    outgoing_ref,
    norm_ref,
    bits_ref,
    queries_ref,
    dq_ref,
    dkv_ref,
    out_w_ref,
    mask_ref,
    reserialized_ref,
    updated_ref,
    logits_ref,
    stats_ref,
    wide_ref,
    arrived,
    placed,
    land_a,
    mid,
    land_b,
    result,
    send_a,
    recv_a,
    send_b,
    recv_b,
    send_c,
    recv_c,
    send_d,
    recv_d,
    send_e,
    recv_e,
):
    scene, seq = lax.axis_index("scene"), lax.axis_index("seq")
    count = queries_ref.shape[0]
    rows = norm_ref.shape[0]
    capacity = 2 * rows // seqs
    chunk = stats_ref.shape[0] // scenes
    piece = chunk // seqs

    def on_scene(offset):
        return lax.rem(scene + offset, scenes)

    def on_seq(offset):
        return lax.rem(seq + offset, seqs)

    barrier = pltpu.get_barrier_semaphore()
    for offset in range(1, scenes):
        pl.semaphore_signal(barrier, inc=1, device_id=(on_scene(offset), seq), device_id_type=MESH)
    for offset in range(1, seqs):
        pl.semaphore_signal(barrier, inc=1, device_id=(scene, on_seq(offset)), device_id_type=MESH)
    pl.semaphore_wait(barrier, scenes + seqs - 2)

    def send(source, dest, out_sem, in_sem, device):
        copy = pltpu.make_async_remote_copy(
            src_ref=source, dst_ref=dest, send_sem=out_sem, recv_sem=in_sem,
            device_id=device, device_id_type=MESH,
        )
        copy.start()
        return copy

    order = sorted(range(1, seqs), key=lambda offset: (abs(offset - seqs // 2), offset))
    first, second = len(order) * 3 // 7, len(order) * 5 // 7
    points = []

    def send_points(offsets):
        for offset in offsets:
            to = on_seq(offset)
            copy = send(outgoing_ref.at[to], arrived.at[offset - 1],
                        send_e.at[offset - 1], recv_e.at[offset - 1], (scene, to))
            points.append((offset, copy))

    send_points(order[:first])
    decoder_kernel(queries_ref, dq_ref, dkv_ref, norm_ref, bits_ref, stats_ref)
    wide_ref[:count] = queries_ref[...].astype(F32)
    if wide_ref.shape[0] > count:
        wide_ref[count:] = jnp.zeros((wide_ref.shape[0] - count, C), F32)
    copies = []
    for offset in range(1, scenes):
        to = on_scene(offset)
        start = pl.multiple_of(to * chunk, 8)
        copies.append(send(stats_ref.at[pl.ds(start, chunk)], land_a.at[offset - 1],
                           send_a.at[offset - 1], recv_a.at[offset - 1], (to, seq)))
    placed[...] = unpack(outgoing_ref[seq], rows, capacity)
    for copy in copies:
        copy.wait()
    mine = stats_ref[pl.ds(pl.multiple_of(scene * chunk, 8), chunk), :]
    summed, total, best = merge([mine] + [land_a[i] for i in range(scenes - 1)])
    lane = iota((chunk, 128), 1)
    stats = jnp.zeros((chunk, 128), F32)
    for head in range(DHEADS):
        stats = jnp.where(lane == head, best[:, head : head + 1], stats)
        stats = jnp.where(lane == DHEADS + head, total[:, head : head + 1], stats)
    mid[:, :C] = summed
    mid[:, C:] = stats
    copies = []
    for offset in range(1, seqs):
        to = on_seq(offset)
        start = pl.multiple_of(to * piece, 8)
        copies.append(send(mid.at[pl.ds(start, piece)], land_b.at[offset - 1],
                           send_b.at[offset - 1], recv_b.at[offset - 1], (scene, to)))
    send_points(order[first:second])
    for copy in copies:
        copy.wait()
    mine = mid[pl.ds(pl.multiple_of(seq * piece, 8), piece), :]
    summed, total, best = merge([mine] + [land_b[i] for i in range(seqs - 1)])
    cross = (summed / spread(total)).astype(BF16)
    place = pl.multiple_of(scene * chunk + seq * piece, 8)
    result[pl.ds(place, piece), :] = layer_norm(wide_ref[pl.ds(place, piece), :] + dot(cross, out_w_ref[...]))
    copies = []
    for offset in range(1, seqs):
        part = result.at[pl.ds(place, piece)]
        copies.append(send(part, part, send_c.at[offset - 1], recv_c.at[offset - 1], (scene, on_seq(offset))))
    send_points(order[second:])
    for copy in copies:
        copy.wait()
    copies = []
    for offset in range(1, scenes):
        part = result.at[pl.ds(pl.multiple_of(scene * chunk, 8), chunk)]
        copies.append(send(part, part, send_d.at[offset - 1], recv_d.at[offset - 1], (on_scene(offset), seq)))
    for offset, copy in points[:first]:
        copy.wait()
        placed[...] += unpack(arrived[offset - 1], rows, capacity)
    for copy in copies:
        copy.wait()
    updated = result[:count]
    updated_ref[...] = updated
    embed = dot(updated.astype(BF16), mask_ref[...]).astype(BF16)
    logits_ref[...] = (dot_t(embed, norm_ref[...]) * (1.0 / math.sqrt(C))).astype(BF16)
    for offset, copy in points[first:-1]:
        copy.wait()
        placed[...] += unpack(arrived[offset - 1], rows, capacity)
    offset, copy = points[-1]
    copy.wait()
    reserialized_ref[...] = (placed[...] + unpack(arrived[offset - 1], rows, capacity)).astype(BF16)


def vmem(n):
    return [pl.BlockSpec(memory_space=pltpu.VMEM)] * n


def body(
    points,
    serial_rank,
    mask_bits,
    qkv_weight,
    proj_weight,
    up_weight,
    down_weight,
    queries,
    dec_q_weight,
    dec_kv_weight,
    dec_out_weight,
    mask_weight,
):
    rows = points.shape[0]
    half = rows // 2
    seqs, scenes = lax.axis_size("seq"), lax.axis_size("scene")
    capacity = 2 * rows // seqs
    count = queries.shape[0]
    params = pltpu.CompilerParams(vmem_limit_bytes=32 * 1024 * 1024)
    prev_half = lax.ppermute(points[half:], "seq", [(i, (i + 1) % seqs) for i in range(seqs)])
    next_half = lax.ppermute(points[:half], "seq", [((i + 1) % seqs, i) for i in range(seqs)])
    smem = pl.BlockSpec(memory_space=pltpu.SMEM)
    kept = [pltpu.VMEM((2, half, C), BF16), pltpu.VMEM((2, 2, half, C), BF16)]
    own = pl.pallas_call(
        own_kernel,
        out_shape=(
            jax.ShapeDtypeStruct((2, half, C), BF16),
            jax.ShapeDtypeStruct((2, 2, half, C), F32),
            jax.ShapeDtypeStruct((2, half, 128), F32),
            jax.ShapeDtypeStruct((2,), F32),
        ),
        in_specs=vmem(2),
        out_specs=tuple(vmem(3)) + (smem,),
        scratch_shapes=kept,
        compiler_params=params,
        cost_estimate=pl.CostEstimate(flops=10**10, bytes_accessed=4 * 10**6, transcendentals=8 * 10**6),
        name="own",
    )(points, qkv_weight)
    normed, outgoing = pl.pallas_call(
        functools.partial(block_kernel, seqs),
        out_shape=(
            jax.ShapeDtypeStruct((rows, C), BF16),
            jax.ShapeDtypeStruct((seqs, capacity + AUX, C), BF16),
        ),
        in_specs=vmem(11) + [smem],
        out_specs=tuple(vmem(2)),
        scratch_shapes=kept
        + [
            pltpu.VMEM((2, 2, half, C), F32),
            pltpu.VMEM((2, 2, half, C), F32),
            pltpu.VMEM((rows, C), BF16),
        ],
        compiler_params=params,
        name="block",
    )(
        points, prev_half, next_half, serial_rank.reshape(1, rows), qkv_weight, proj_weight, up_weight, down_weight, *own
    )
    piece = -(-count // (8 * seqs * scenes)) * 8
    padded = piece * seqs * scenes
    return pl.pallas_call(
        functools.partial(tail_kernel, scenes, seqs),
        out_shape=(
            jax.ShapeDtypeStruct((rows, C), BF16),
            jax.ShapeDtypeStruct((count, C), F32),
            jax.ShapeDtypeStruct((count, rows), BF16),
        ),
        in_specs=vmem(8),
        out_specs=tuple(vmem(3)),
        scratch_shapes=[
            pltpu.VMEM((padded, STATS), F32),
            pltpu.VMEM((padded, C), F32),
            pltpu.VMEM((seqs - 1, capacity + AUX, C), BF16),
            pltpu.VMEM((rows, C), F32),
            pltpu.VMEM((scenes - 1, padded // scenes, STATS), F32),
            pltpu.VMEM((padded // scenes, STATS), F32),
            pltpu.VMEM((seqs - 1, piece, STATS), F32),
            pltpu.VMEM((padded, C), F32),
        ]
        + [
            pltpu.SemaphoreType.DMA((n - 1,))
            for n in (scenes, scenes, seqs, seqs, seqs, seqs, scenes, scenes, seqs, seqs)
        ],
        compiler_params=pltpu.CompilerParams(
            collective_id=0, has_side_effects=True, vmem_limit_bytes=32 * 1024 * 1024
        ),
        name="tail",
    )(outgoing, normed, mask_bits, queries, dec_q_weight, dec_kv_weight, dec_out_weight, mask_weight)


def solution(mesh):
    split = ("scene", "seq")
    in_specs = (P(split, None), P(split), P(None, split)) + (P(),) * 9
    out_specs = (P(split, None), P(), P(None, split))
    return jax.shard_map(body, mesh=mesh, in_specs=in_specs, out_specs=out_specs, check_vma=False)
```
